768 devices in a mesh: dp: 32 (over z_lo, y), seq: 24 (over z_hi, x, core).
Axes of the slice: x: 4, y: 8, z: 12 (z_hi: 3, z_lo: 4; z = z_hi * 4 + z_lo), core: 2. Of those that a mesh axis runs over, the one named last changes fastest.
Arguments:
- queries: bfloat16 [32, 3072, 6144], P('dp', 'seq'), may hold values from -6 to 6
- keys: bfloat16 [32, 3072, 768], P('dp', 'seq'), may hold values from -6 to 6
- values: bfloat16 [32, 3072, 768], P('dp', 'seq'), may hold values from -6 to 6
- segments: int32 [32, 3072], P('dp'), may hold values from 0 to 11, never falling along the last dimension, each value on 1 to 384 neighbouring positions
Outputs:
- attended: bfloat16 [32, 3072, 6144], P('dp', 'seq')
- query_factor: float32 [48], replicated
- key_head_factor: float32 [6], replicated
The draws below stay inside these ranges and needn't reach their ends.
Inputs may be any that keep to these rules, and one draw needn't show every extreme that they name: `segments`: each row's ids never fall; a document holds at most 384 positions, and some document holds exactly 384.
All inputs are finite; a program needn't handle non-finite values.
Results may differ from the reference program's by a relative error of at most 0.0046.
Values may be sent and summed in bfloat16 or wider, within the bound.
A program may use at most 32 MiB of HBM per device.

```python
import math
import jax
import jax.numpy as jnp
import numpy as np
from jax import lax

QUERY_HEADS = 48
KEY_VALUE_HEADS = 6
HEAD_SIZE = 128
BATCH_SEQUENCES = 32
PACKED_LENGTH = 3072
DOCS = 12
DOCUMENT_LIMIT = 384


def draw_queries(key, part):
    random_seed_key = jax.random.fold_in(key, 11)
    scale_key = jax.random.fold_in(key, 13)
    head_scale = jnp.exp(jax.random.uniform(scale_key, (QUERY_HEADS,), jnp.float32, math.log(0.4), math.log(2.0)))
    noise = jnp.clip(jax.random.normal(random_seed_key, (BATCH_SEQUENCES, PACKED_LENGTH, QUERY_HEADS, HEAD_SIZE), jnp.float32), -3.0, 3.0)
    final_output = noise * head_scale[:, None]
    return final_output.reshape(BATCH_SEQUENCES, PACKED_LENGTH, QUERY_HEADS * HEAD_SIZE).astype(jnp.bfloat16)


def draw_keys(key, part):
    random_seed_key = jax.random.fold_in(key, 17)
    final_output = jnp.clip(jax.random.normal(random_seed_key, (BATCH_SEQUENCES, PACKED_LENGTH, KEY_VALUE_HEADS, HEAD_SIZE), jnp.float32), -3.0, 3.0)
    return final_output.reshape(BATCH_SEQUENCES, PACKED_LENGTH, KEY_VALUE_HEADS * HEAD_SIZE).astype(jnp.bfloat16)


def shard_levels(key, dims, cuts, smallest, top_value):
    factor_of, own = 1.0, jax.random.fold_in(key, 6)
    for dim, shards_of in cuts:
        draws = jnp.exp(jax.random.uniform(jax.random.fold_in(own, dim), (shards_of,), jnp.float32, smallest / len(cuts), top_value / len(cuts)))
        factor_of = factor_of * jnp.repeat(draws, dims[dim] // shards_of).reshape([-1 if axis == dim else 1 for axis in range(len(dims))])
    return factor_of


def length_profile(count, total, bound, skew):
    loads = [(1 << 20) // math.isqrt(standing ** skew) + 1 for standing in range(2, count + 1)]
    surplus, holding = total - bound - (count - 1), [1] * (count - 1)
    while surplus > 0:
        candidates = [i for i in range(count - 1) if holding[i] < bound]
        whole, budget = sum([loads[i] for i in candidates]), surplus
        for i in candidates:
            extra = min(bound - holding[i], max(1, budget * loads[i] // whole), surplus)
            holding[i] = holding[i] + extra
            surplus = surplus - extra
    return np.array([bound] + holding)


def uneven(key, count, total, most, skew):
    if count == 2:
        one = jax.random.randint(key, (), max(1, total - most), min(most, total - 1) + 1)
        return jnp.stack([one, total - one])
    tallies = jnp.asarray(length_profile(count, total, most, skew), jnp.int32)
    couples = (count - 1) // 2
    giver, receiver = tallies[1:1 + 2 * couples:2], tallies[2:2 + 2 * couples:2]
    room = jnp.minimum(giver - 1, most - receiver)
    passed = jax.random.randint(jax.random.fold_in(key, 1), (couples,), 0, 1 << 20) % (room + 1)
    tallies = tallies.at[1:1 + 2 * couples:2].set(giver - passed).at[2:2 + 2 * couples:2].set(receiver + passed)
    return tallies[jax.random.permutation(jax.random.fold_in(key, 2), count)]


def scatter_about(own_key, dims, spread, most, cuts=(), kind=jnp.bfloat16):
    values = spread * jax.random.normal(own_key, dims, jnp.float32)
    if cuts:
        values = values * shard_levels(own_key, dims, cuts, -0.22, 0.18)
    return jnp.clip(values, -most, most).astype(kind)


def setup_inputs(seed: int = 0) -> dict:
    seeds = jax.random.split(jax.random.key(seed), 5)
    queries = draw_queries(jax.random.fold_in(seeds[4], 71), 0)
    keys = draw_keys(jax.random.fold_in(seeds[4], 71), 0)
    values = scatter_about(seeds[2], (BATCH_SEQUENCES, PACKED_LENGTH, KEY_VALUE_HEADS * HEAD_SIZE), 1.0, 6.0, ((0, 32), (1, 24)))
    segments = jax.vmap(lambda own: jnp.searchsorted(jnp.cumsum(uneven(own, DOCS, PACKED_LENGTH, DOCUMENT_LIMIT, 1)), jnp.arange(PACKED_LENGTH), side="right"))(jax.random.split(seeds[3], BATCH_SEQUENCES)).reshape((BATCH_SEQUENCES, PACKED_LENGTH)).astype(jnp.int32)
    return {"queries": queries, "keys": keys, "values": values, "segments": segments}


clip_level = 6.0

def attend(query_block, key_block, value_block, query_pos, key_pos, doc_ids):
    scale = query_block.shape[-1] ** (-0.5)
    logits = jnp.einsum('qcgd,kcd->cgqk', query_block.astype(jnp.float32), key_block.astype(jnp.float32)) * scale
    query_doc = jnp.take(doc_ids, query_pos)
    key_doc = jnp.take(doc_ids, jnp.maximum(key_pos, 0))
    valid = (key_pos[None, :] <= query_pos[:, None]) & (key_pos[None, :] >= 0) & (key_doc[None, :] == query_doc[:, None])
    logits = jnp.where(valid, logits, -1e+30)
    largest = lax.optimization_barrier(jnp.max(logits, axis=-1, keepdims=True))
    expo = jnp.exp(logits - largest)
    total = lax.optimization_barrier(jnp.sum(expo, axis=-1, keepdims=True))
    weights = (expo / total).astype(jnp.bfloat16)
    mixed = jnp.einsum('cgqk,kcd->qcgd', weights.astype(jnp.float32), value_block.astype(jnp.float32)).astype(jnp.bfloat16)
    return (mixed, lax.optimization_barrier(jnp.max(largest[..., 0], axis=-1)))

def clip_factors(head_max):
    query_group = QUERY_HEADS // KEY_VALUE_HEADS
    clipped_logits = clip_level / jnp.maximum(head_max, clip_level)
    key_head_factor = jnp.sqrt(lax.optimization_barrier(jnp.min(clipped_logits.reshape(KEY_VALUE_HEADS, query_group), axis=1)))
    query_factor = clipped_logits / jnp.repeat(key_head_factor, query_group)
    return (query_factor, key_head_factor)

def reference(queries, keys, values, segments):
    query_group = QUERY_HEADS // KEY_VALUE_HEADS
    block = min(512, PACKED_LENGTH)
    blocks = PACKED_LENGTH // block

    def one_row(items):
        query_row_vector, key_row_vector, value_row_vector, doc_ids = items
        query_head_list = query_row_vector.reshape(PACKED_LENGTH, KEY_VALUE_HEADS, query_group, HEAD_SIZE)
        leading_part = jnp.zeros((DOCUMENT_LIMIT, KEY_VALUE_HEADS, HEAD_SIZE), jnp.bfloat16)
        key_padding = jnp.concatenate([leading_part, key_row_vector.reshape(PACKED_LENGTH, KEY_VALUE_HEADS, HEAD_SIZE)], axis=0)
        value_padding = jnp.concatenate([leading_part, value_row_vector.reshape(PACKED_LENGTH, KEY_VALUE_HEADS, HEAD_SIZE)], axis=0)
        pieces = []
        maxima = []
        for number in range(blocks):
            start = number * block
            query_pos = jnp.arange(block, dtype=jnp.int32) + start
            key_pos = jnp.arange(block + DOCUMENT_LIMIT, dtype=jnp.int32) + (start - DOCUMENT_LIMIT)
            mixed, largest = attend(query_head_list[start:start + block], key_padding[start:start + block + DOCUMENT_LIMIT], value_padding[start:start + block + DOCUMENT_LIMIT], query_pos, key_pos, doc_ids)
            pieces.append(mixed.reshape(block, QUERY_HEADS * HEAD_SIZE))
            maxima.append(largest.reshape(QUERY_HEADS))
        return (jnp.concatenate(pieces, axis=0), lax.optimization_barrier(jnp.max(jnp.stack(maxima), axis=0)))
    attended, row_max = lax.map(one_row, (queries, keys, values, segments))
    query_factor, key_head_factor = clip_factors(lax.optimization_barrier(jnp.max(row_max, axis=0)))
    return (attended, query_factor, key_head_factor)
```

```python
import functools
import math

import jax
import jax.numpy as jnp
from jax import lax
from jax.experimental import pallas as pl
from jax.experimental.pallas import tpu as pltpu
from jax.sharding import PartitionSpec as P

QUERY_HEADS = 48
KV_HEADS = 6
GROUP = QUERY_HEADS // KV_HEADS
HEAD = 128
ROWS = 128
CLIP = 6.0
NEG = -1e30
SCALE = HEAD**-0.5
CHUNKS = 2
CROWS = ROWS // CHUNKS
MESH = pl.DeviceIdType.MESH
BF16, F32 = jnp.bfloat16, jnp.float32

F1, F2, F34, F5, CROSS, RELAY, RELAY2 = range(7)
R1, R2, R3, RB = range(4)


def kernel(
    q_hbm, k_hbm, v_hbm, seg_ref, out_hbm, fac_ref,
    q_ref, kall, vall, relay, bias_ref, s_ref, rm_ref, p_ref, o_ref, hm_ref,
    ar_a, ar_b, ar_c,
    load_sem, out_sem, send_sem, recv_sem, a_send, a_recv, b_send, b_recv, c_send, c_recv,
):
    dp, s = lax.axis_index("dp"), lax.axis_index("seq")
    core = lax.rem(s, 2)
    r8 = lax.rem(s, 8)
    zh = lax.div(s, 8)
    x = lax.div(r8, 2)
    y = lax.rem(dp, 8)
    zl = lax.div(dp, 8)
    z = zh * 4 + zl

    def dev_a(k):
        return (dp, zh * 8 + lax.rem(r8 + k, 8))

    def dev_b(k):
        return (zl * 8 + lax.rem(y + k, 8), s)

    def dev_c(k):
        zz = lax.rem(z + k, 12)
        return (lax.rem(zz, 4) * 8 + y, lax.div(zz, 4) * 8 + r8)

    barrier = pltpu.get_barrier_semaphore()
    for n, dev in ((8, dev_a), (8, dev_b), (12, dev_c)):
        for k in range(1, n):
            pl.semaphore_signal(barrier, inc=1, device_id=dev(k), device_id_type=MESH)

    load_k = pltpu.make_async_copy(k_hbm, kall.at[pl.ds(3 * ROWS, ROWS)], load_sem.at[0])
    load_q = pltpu.make_async_copy(q_hbm, q_ref, load_sem.at[1])
    load_v = pltpu.make_async_copy(v_hbm, vall.at[pl.ds(3 * ROWS, ROWS)], load_sem.at[2])
    load_k.start()
    load_q.start()
    load_v.start()

    for d in (1, 2, 3):
        @pl.when(s < d)
        def _():
            zero = jnp.zeros((ROWS, KV_HEADS * HEAD), BF16)
            kall[pl.ds((3 - d) * ROWS, ROWS), :] = zero
            vall[pl.ds((3 - d) * ROWS, ROWS), :] = zero

    def seg_row(block):
        start = pl.multiple_of(jnp.maximum(block, 0) * ROWS, ROWS)
        return seg_ref[:, pl.ds(start, ROWS)].astype(F32)

    own = jnp.broadcast_to(seg_row(s), (ROWS, ROWS))
    query_doc = jnp.transpose(own)
    row = lax.broadcasted_iota(jnp.int32, (ROWS, ROWS), 0)
    col = lax.broadcasted_iota(jnp.int32, (ROWS, ROWS), 1)
    for t in range(4):
        key_doc = jnp.broadcast_to(seg_row(s - 3 + t), (ROWS, ROWS))
        gap = jnp.abs(key_doc - query_doc)
        if t == 3:
            gap = gap + jnp.maximum(col - row, 0).astype(F32)
        else:
            gap = gap + jnp.where(s - 3 + t < 0, 1.0, 0.0)
        bias_ref[t] = jnp.where(gap > 0.5, NEG, 0.0)
    hm_ref[...] = jnp.full((ROWS, ROWS), NEG, F32)

    def s_block(t, last):
        def body(c, carry):
            base = c * (GROUP * HEAD)
            qc = jnp.concatenate(
                [
                    q_ref[:, pl.ds(pl.multiple_of(base + g * HEAD, HEAD), HEAD)]
                    for g in range(GROUP)
                ],
                axis=0,
            )
            kb = kall[pl.ds(t * ROWS, ROWS), pl.ds(pl.multiple_of(c * HEAD, HEAD), HEAD)]
            lg = lax.dot_general(qc, kb, (((1,), (1,)), ((), ())), preferred_element_type=F32)
            lg = lg.reshape(GROUP, ROWS, ROWS) + bias_ref[t][None]
            s_ref[c, t] = lg.reshape(GROUP * ROWS, ROWS)
            mx = lg
            if t != 3:
                mx = jnp.maximum(mx, rm_ref[c].reshape(GROUP, ROWS, ROWS))
            rm_ref[c] = mx.reshape(GROUP * ROWS, ROWS)
            if last:
                hm_ref[pl.ds(pl.multiple_of(c * GROUP, GROUP), GROUP), :] = jnp.max(mx, axis=1)
            return carry

        lax.fori_loop(0, KV_HEADS, body, 0)

    load_k.wait()
    load_q.wait()
    s_block(3, False)
    load_v.wait()
    pl.semaphore_wait(barrier, 25)

    bufs = (kall, vall)

    def part(i, d, h):
        return bufs[i].at[pl.ds((3 - d) * ROWS + h * CROWS, CROWS)]

    def relay_part(i, h):
        return relay.at[i, pl.ds(h * CROWS, CROWS)]

    def copy(src, dst, kind, slot, i, h, target):
        return pltpu.make_async_remote_copy(
            src_ref=src,
            dst_ref=dst,
            send_sem=send_sem.at[kind, i, h],
            recv_sem=recv_sem.at[slot, i, h],
            device_id=(dp, target),
            device_id_type=MESH,
        )

    def await_part(slot, i, h):
        dst = relay_part(i, h) if slot == RB else part(i, slot + 1, h)
        copy(dst, dst, F1, slot, i, h, s).wait_recv()

    odd, even = core == 1, core == 0
    flows = {
        "f1": (even, lambda i, h: copy(part(i, 0, h), part(i, 1, h), F1, R1, i, h, s + 1)),
        "f2": (x <= 2, lambda i, h: copy(part(i, 0, h), part(i, 2, h), F2, R2, i, h, s + 2)),
        "f3": (even & (s >= 2), lambda i, h: copy(part(i, 2, h), part(i, 3, h), F34, R3, i, h, s + 1)),
        "f4": (odd & (s >= 2), lambda i, h: copy(part(i, 2, h), part(i, 1, h), F34, R1, i, h, s - 1)),
        "f5": (
            odd & (x >= 1) & (x <= 2),
            lambda i, h: copy(part(i, 2, h), part(i, 3, h), F5, R3, i, h, s + 1),
        ),
        "cross_z": (
            odd & (x >= 2) & (zh <= 1),
            lambda i, h: copy(part(i, 0, h), relay_part(i, h), CROSS, RB, i, h, s + 8),
        ),
        "cross_x": (
            even & (x == 3) & (zh <= 1),
            lambda i, h: copy(part(i, 0, h), relay_part(i, h), CROSS, RB, i, h, s - 6),
        ),
        "relay_z": (
            even & (x == 0) & (zh <= 1),
            lambda i, h: copy(relay_part(i, h), part(i, 2, h), RELAY, R2, i, h, s + 8),
        ),
        "relay_3": (
            odd & (x == 3) & (zh >= 1),
            lambda i, h: copy(relay_part(i, h), part(i, 2, h), RELAY, R2, i, h, s - 6),
        ),
        "relay_3b": (
            odd & (x == 3) & (zh >= 1),
            lambda i, h: copy(relay_part(i, h), part(i, 3, h), RELAY2, R3, i, h, s - 5),
        ),
        "relay_2": (
            odd & (x == 2) & (zh >= 1),
            lambda i, h: copy(relay_part(i, h), part(i, 3, h), RELAY, R3, i, h, s - 5),
        ),
    }

    def start(name, i, h=None, also=None):
        cond, make = flows[name]
        if also is not None:
            cond = cond & also

        @pl.when(cond)
        def _():
            for j in range(CHUNKS) if h is None else (h,):
                make(i, j).start()

    K, V = 0, 1
    start("cross_z", K)
    start("cross_x", K)
    start("f2", K)
    start("f1", K)
    start("cross_z", V)
    start("cross_x", V)
    start("f2", V, also=x == 0)
    start("f1", V)

    @pl.when(flows["relay_z"][0])
    def _():
        for i in (K, V):
            for h in range(CHUNKS):
                await_part(RB, i, h)
                flows["relay_z"][1](i, h).start()

    def take_two(i):
        for h in range(CHUNKS):
            @pl.when(s >= 2)
            def _():
                await_part(R2, i, h)
            start("f4", i, h)
            start("f3", i, h)
            start("f5", i, h)

    def take(slot, i):
        @pl.when(s >= slot + 1)
        def _():
            for h in range(CHUNKS):
                await_part(slot, i, h)

    def take_relay(i):
        for h in range(CHUNKS):
            @pl.when(odd & (x >= 2) & (zh >= 1))
            def _():
                await_part(RB, i, h)
            start("relay_3", i, h)
            start("relay_3b", i, h)
            start("relay_2", i, h)

    take_two(K)
    start("f2", V, also=x > 0)
    s_block(1, False)
    take(R1, K)
    s_block(2, False)
    take(R3, K)
    s_block(0, True)

    def ar_copies(buf, n, dev, sends, recvs):
        return [
            pltpu.make_async_remote_copy(
                src_ref=buf.at[0],
                dst_ref=buf.at[k],
                send_sem=sends.at[k],
                recv_sem=recvs.at[k],
                device_id=dev(k),
                device_id_type=MESH,
            )
            for k in range(1, n)
        ]

    def ar_finish(buf, copies):
        for c in copies:
            c.wait_recv()
        return jnp.max(buf[...], axis=0)

    stage_a = ar_copies(ar_a, 8, dev_a, a_send, a_recv)
    stage_b = ar_copies(ar_b, 8, dev_b, b_send, b_recv)
    stage_c = ar_copies(ar_c, 12, dev_c, c_send, c_recv)

    ar_a[0] = jnp.max(jnp.transpose(hm_ref[...]), axis=0, keepdims=True) * SCALE
    for c in stage_a:
        c.start()
    take_relay(K)

    def p_body(c, carry):
        m = jnp.max(rm_ref[c], axis=1, keepdims=True)
        for t in range(4):
            p = jnp.exp2((s_ref[c, t] - m) * (SCALE * math.log2(math.e)))
            p_ref[c, :, t * ROWS : (t + 1) * ROWS] = p.astype(BF16)
        return carry

    lax.fori_loop(0, KV_HEADS, p_body, 0)

    def out_copy(c):
        cols = pl.ds(c * GROUP * HEAD, GROUP * HEAD)
        return pltpu.make_async_copy(o_ref.at[:, cols], out_hbm.at[:, cols], out_sem.at[c])

    def finish_values():
        take_two(V)
        take(R1, V)
        take(R3, V)
        for c in range(KV_HEADS):
            vc = jnp.concatenate(
                [vall[:, c * HEAD : (c + 1) * HEAD], jnp.ones((4 * ROWS, HEAD), BF16)], axis=1
            )
            acc = jnp.dot(p_ref[c], vc, preferred_element_type=F32)
            o = (acc[:, :HEAD] / acc[:, HEAD:]).astype(BF16)
            for g in range(GROUP):
                h = c * GROUP + g
                o_ref[:, h * HEAD : (h + 1) * HEAD] = o[g * ROWS : (g + 1) * ROWS]
            out_copy(c).start()

    late = (s >= 8) & (r8 <= 2)

    @pl.when(jnp.logical_not(late))
    def _():
        finish_values()

    ar_b[0] = ar_finish(ar_a, stage_a)
    for c in stage_b:
        c.start()
    take_relay(V)
    ar_c[0] = ar_finish(ar_b, stage_b)
    for c in stage_c:
        c.start()

    @pl.when(late)
    def _():
        finish_values()

    head_max = ar_finish(ar_c, stage_c)
    clipped = CLIP / jnp.maximum(head_max, CLIP)
    spread = jnp.broadcast_to(clipped, (ROWS, ROWS))
    down = jnp.transpose(spread)
    group = lax.div(row, GROUP)
    big = jnp.full((ROWS, ROWS), jnp.inf, F32)
    per_query = jnp.min(jnp.where(group == lax.div(col, GROUP), down, big), axis=0, keepdims=True)
    per_key = jnp.min(
        jnp.where(group == jnp.minimum(col, KV_HEADS - 1), down, big), axis=0, keepdims=True
    )
    fac_ref[0:1, :] = clipped / jnp.sqrt(per_query)
    fac_ref[1:2, :] = jnp.sqrt(per_key)

    for copies in (stage_a, stage_b, stage_c):
        for c in copies:
            c.wait_send()
    for cond, make in flows.values():
        @pl.when(cond)
        def _():
            for i in (K, V):
                for h in range(CHUNKS):
                    make(i, h).wait_send()
    for c in range(KV_HEADS):
        out_copy(c).wait()


def local(queries, keys, values, segments):
    width, kv_width = QUERY_HEADS * HEAD, KV_HEADS * HEAD
    any_spec = pl.BlockSpec(memory_space=pl.ANY)
    vmem_spec = pl.BlockSpec(memory_space=pltpu.VMEM)
    dma = pltpu.SemaphoreType.DMA
    attended, factors = pl.pallas_call(
        kernel,
        name="packed_attention",
        out_shape=(
            jax.ShapeDtypeStruct((ROWS, width), BF16),
            jax.ShapeDtypeStruct((2, ROWS), F32),
        ),
        in_specs=[any_spec, any_spec, any_spec, vmem_spec],
        out_specs=(any_spec, vmem_spec),
        scratch_shapes=[
            pltpu.VMEM((ROWS, width), BF16),
            pltpu.VMEM((4 * ROWS, kv_width), BF16),
            pltpu.VMEM((4 * ROWS, kv_width), BF16),
            pltpu.VMEM((2, ROWS, kv_width), BF16),
            pltpu.VMEM((4, ROWS, ROWS), F32),
            pltpu.VMEM((KV_HEADS, 4, GROUP * ROWS, ROWS), F32),
            pltpu.VMEM((KV_HEADS, GROUP * ROWS, ROWS), F32),
            pltpu.VMEM((KV_HEADS, GROUP * ROWS, 4 * ROWS), BF16),
            pltpu.VMEM((ROWS, width), BF16),
            pltpu.VMEM((ROWS, ROWS), F32),
            pltpu.VMEM((8, 1, ROWS), F32),
            pltpu.VMEM((8, 1, ROWS), F32),
            pltpu.VMEM((12, 1, ROWS), F32),
            dma((3,)),
            dma((KV_HEADS,)),
            dma((7, 2, CHUNKS)),
            dma((4, 2, CHUNKS)),
            dma((8,)),
            dma((8,)),
            dma((8,)),
            dma((8,)),
            dma((12,)),
            dma((12,)),
        ],
        compiler_params=pltpu.CompilerParams(
            collective_id=0, has_side_effects=True, vmem_limit_bytes=48 * 1024 * 1024
        ),
    )(queries[0], keys[0], values[0], segments)
    return attended[None], factors[0, :QUERY_HEADS], factors[1, :KV_HEADS]


def solution(mesh):
    in_specs = (P("dp", "seq", None), P("dp", "seq", None), P("dp", "seq", None), P("dp", None))
    out_specs = (P("dp", "seq", None), P(), P())
    return jax.shard_map(local, mesh=mesh, in_specs=in_specs, out_specs=out_specs, check_vma=False)
```

```python
import functools
import math

import jax
import jax.numpy as jnp
from jax import lax
from jax.experimental import pallas as pl
from jax.experimental.pallas import tpu as pltpu
from jax.sharding import PartitionSpec as P

QUERY_HEADS = 48
KV_HEADS = 6
GROUP = QUERY_HEADS // KV_HEADS
HEAD = 128
ROWS = 128
CLIP = 6.0
NEG = -1e30
SCALE = HEAD**-0.5
CHUNKS = 2
CROWS = ROWS // CHUNKS
MESH = pl.DeviceIdType.MESH
BF16, F32 = jnp.bfloat16, jnp.float32

F1, F2, F34, F5, CROSS, RELAY = range(6)
R1, R2, R3, RB = range(4)


def kernel(
    q_hbm, k_hbm, v_hbm, seg_hbm, o_ref, fac_ref,
    q_ref, kall, vall, relay, bias_ref, s_ref, rm_ref, p_ref, seg_ref, hm_ref,
    ar_a, ar_b, ar_c,
    load_sem, send_sem, recv_sem, a_send, a_recv, b_send, b_recv, c_send, c_recv,
):
    dp, s = lax.axis_index("dp"), lax.axis_index("seq")
    core = lax.rem(s, 2)
    r8 = lax.rem(s, 8)
    zh = lax.div(s, 8)
    x = lax.div(r8, 2)
    y = lax.rem(dp, 8)
    zl = lax.div(dp, 8)
    z = zh * 4 + zl

    def dev_a(k):
        return (dp, zh * 8 + lax.rem(r8 + k, 8))

    def dev_b(k):
        return (zl * 8 + lax.rem(y + k, 8), s)

    def dev_c(k):
        zz = lax.rem(z + k, 12)
        return (lax.rem(zz, 4) * 8 + y, lax.div(zz, 4) * 8 + r8)

    load_seg = pltpu.make_async_copy(seg_hbm, seg_ref, load_sem.at[3])
    load_seg.start()
    barrier = pltpu.get_barrier_semaphore()
    for n, dev in ((8, dev_a), (8, dev_b), (12, dev_c)):
        for k in range(1, n):
            pl.semaphore_signal(barrier, inc=1, device_id=dev(k), device_id_type=MESH)

    @pl.when((x == 0) & (zh >= 1))
    def _():
        source = (dp, s - jnp.where(core == 0, 3, 2))
        pl.semaphore_signal(barrier, inc=1, device_id=source, device_id_type=MESH)

    load_k = pltpu.make_async_copy(k_hbm, kall.at[pl.ds(3 * ROWS, ROWS)], load_sem.at[0])
    load_q = pltpu.make_async_copy(q_hbm, q_ref, load_sem.at[1])
    load_v = pltpu.make_async_copy(v_hbm, vall.at[pl.ds(3 * ROWS, ROWS)], load_sem.at[2])
    load_k.start()
    load_q.start()
    load_v.start()

    for d in (1, 2, 3):
        @pl.when(s < d)
        def _():
            zero = jnp.zeros((ROWS, KV_HEADS * HEAD), BF16)
            kall[pl.ds((3 - d) * ROWS, ROWS), :] = zero
            vall[pl.ds((3 - d) * ROWS, ROWS), :] = zero

    load_seg.wait()

    def seg_row(block):
        start = pl.multiple_of(jnp.maximum(block, 0) * ROWS, ROWS)
        return seg_ref[:, pl.ds(start, ROWS)].astype(F32)

    own = jnp.broadcast_to(seg_row(s), (ROWS, ROWS))
    query_doc = jnp.transpose(own)
    row = lax.broadcasted_iota(jnp.int32, (ROWS, ROWS), 0)
    col = lax.broadcasted_iota(jnp.int32, (ROWS, ROWS), 1)
    for t in range(4):
        key_doc = jnp.broadcast_to(seg_row(s - 3 + t), (ROWS, ROWS))
        gap = jnp.abs(key_doc - query_doc)
        if t == 3:
            gap = gap + jnp.maximum(col - row, 0).astype(F32)
        else:
            gap = gap + jnp.where(s - 3 + t < 0, 1.0, 0.0)
        bias_ref[t] = jnp.where(gap > 0.5, NEG, 0.0)
    hm_ref[...] = jnp.full((ROWS, ROWS), NEG, F32)

    def s_blocks(first, count, last):
        def body(c, carry):
            base = c * (GROUP * HEAD)
            qc = jnp.concatenate(
                [
                    q_ref[:, pl.ds(pl.multiple_of(base + g * HEAD, HEAD), HEAD)]
                    for g in range(GROUP)
                ],
                axis=0,
            )
            cols = pl.ds(pl.multiple_of(c * HEAD, HEAD), HEAD)
            kb = kall[pl.ds(first * ROWS, count * ROWS), cols]
            lg = lax.dot_general(qc, kb, (((1,), (1,)), ((), ())), preferred_element_type=F32)
            mx = None if first == 3 else rm_ref[c].reshape(GROUP, ROWS, ROWS)
            for n in range(count):
                t = first + n
                one = lg[:, n * ROWS : (n + 1) * ROWS].reshape(GROUP, ROWS, ROWS)
                one = one + bias_ref[t][None]
                s_ref[c, t] = one.reshape(GROUP * ROWS, ROWS)
                mx = one if mx is None else jnp.maximum(mx, one)
            rm_ref[c] = mx.reshape(GROUP * ROWS, ROWS)
            if last:
                hm_ref[pl.ds(pl.multiple_of(c * GROUP, GROUP), GROUP), :] = jnp.max(mx, axis=1)
            return carry

        lax.fori_loop(0, KV_HEADS, body, 0)

    load_k.wait()
    load_q.wait()
    s_blocks(3, 1, False)
    load_v.wait()
    direct = (core == 1) & (x >= 2) & (zh <= 1)
    pl.semaphore_wait(barrier, 25 + jnp.where(direct, 1, 0))

    bufs = (kall, vall)

    def part(i, d, h):
        return bufs[i].at[pl.ds((3 - d) * ROWS + h * CROWS, CROWS)]

    def relay_part(i, h):
        return relay.at[i, pl.ds(h * CROWS, CROWS)]

    def copy(src, dst, kind, slot, i, h, target):
        return pltpu.make_async_remote_copy(
            src_ref=src,
            dst_ref=dst,
            send_sem=send_sem.at[kind, i, h],
            recv_sem=recv_sem.at[slot, i, h],
            device_id=(dp, target),
            device_id_type=MESH,
        )

    def await_part(slot, i, h):
        dst = relay_part(i, h) if slot == RB else part(i, slot + 1, h)
        copy(dst, dst, F1, slot, i, h, s).wait_recv()

    odd, even = core == 1, core == 0
    flows = {
        "f1": (even, lambda i, h: copy(part(i, 0, h), part(i, 1, h), F1, R1, i, h, s + 1)),
        "f2": (x <= 2, lambda i, h: copy(part(i, 0, h), part(i, 2, h), F2, R2, i, h, s + 2)),
        "f3": (even & (s >= 2), lambda i, h: copy(part(i, 2, h), part(i, 3, h), F34, R3, i, h, s + 1)),
        "f4": (odd & (s >= 2), lambda i, h: copy(part(i, 2, h), part(i, 1, h), F34, R1, i, h, s - 1)),
        "f5": (
            odd & (s >= 3) & (x <= 2),
            lambda i, h: copy(part(i, 2, h), part(i, 3, h), F5, R3, i, h, s + 1),
        ),
        "cross_7": (
            odd & (x == 3) & (zh <= 1),
            lambda i, h: copy(part(i, 0, h), part(i, 2, h), CROSS, R2, i, h, s + 2),
        ),
        "cross_5": (
            odd & (x == 2) & (zh <= 1),
            lambda i, h: copy(part(i, 0, h), part(i, 3, h), CROSS, R3, i, h, s + 3),
        ),
        "cross_6": (
            even & (x == 3) & (zh <= 1),
            lambda i, h: copy(part(i, 0, h), relay_part(i, h), CROSS, RB, i, h, s - 6),
        ),
        "relay_6": (
            even & (x == 0) & (zh <= 1),
            lambda i, h: copy(relay_part(i, h), part(i, 2, h), RELAY, R2, i, h, s + 8),
        ),
    }

    def start(name, i, h=None, also=None):
        cond, make = flows[name]
        if also is not None:
            cond = cond & also

        @pl.when(cond)
        def _():
            for j in range(CHUNKS) if h is None else (h,):
                make(i, j).start()

    K, V = 0, 1

    def cross(i):
        start("cross_7", i)
        start("cross_5", i)
        start("cross_6", i)

    def take_relay(i, also):
        for h in range(CHUNKS):
            @pl.when(flows["relay_6"][0] & also)
            def _():
                await_part(RB, i, h)
                flows["relay_6"][1](i, h).start()

    cross(K)
    start("f2", K)
    start("f1", K)
    start("f2", V, also=x == 0)
    start("f1", V, also=x == 0)
    take_relay(K, zh >= 0)
    take_relay(V, zh >= 1)

    def take_two(i):
        for h in range(CHUNKS):
            @pl.when(s >= 2)
            def _():
                await_part(R2, i, h)
            start("f4", i, h)
            start("f3", i, h)
            start("f5", i, h)

    def take(slot, i):
        @pl.when(s >= slot + 1)
        def _():
            for h in range(CHUNKS):
                await_part(slot, i, h)

    take_two(K)
    start("f2", V, also=x > 0)
    start("f1", V, also=x > 0)
    take(R1, K)
    s_blocks(1, 2, False)
    cross(V)
    take(R3, K)
    s_blocks(0, 1, True)

    def ar_copies(buf, n, dev, sends, recvs):
        return [
            pltpu.make_async_remote_copy(
                src_ref=buf.at[0],
                dst_ref=buf.at[k],
                send_sem=sends.at[k],
                recv_sem=recvs.at[k],
                device_id=dev(k),
                device_id_type=MESH,
            )
            for k in range(1, n)
        ]

    def ar_finish(buf, copies):
        for c in copies:
            c.wait_recv()
        return jnp.max(buf[...], axis=0)

    stage_a = ar_copies(ar_a, 8, dev_a, a_send, a_recv)
    stage_b = ar_copies(ar_b, 8, dev_b, b_send, b_recv)
    stage_c = ar_copies(ar_c, 12, dev_c, c_send, c_recv)

    ar_a[0] = jnp.max(jnp.transpose(hm_ref[...]), axis=0, keepdims=True) * SCALE
    for c in stage_a:
        c.start()
    take_relay(V, zh < 1)

    def p_body(c, carry):
        m = jnp.max(rm_ref[c], axis=1, keepdims=True)
        for t in range(4):
            p = jnp.exp2((s_ref[c, t] - m) * (SCALE * math.log2(math.e)))
            p_ref[c, :, t * ROWS : (t + 1) * ROWS] = p.astype(BF16)
        return carry

    lax.fori_loop(0, KV_HEADS, p_body, 0)

    def finish_values():
        take(R1, V)
        take(R3, V)
        for c in range(KV_HEADS):
            vc = jnp.concatenate(
                [vall[:, c * HEAD : (c + 1) * HEAD], jnp.ones((4 * ROWS, HEAD), BF16)], axis=1
            )
            acc = jnp.dot(p_ref[c], vc, preferred_element_type=F32)
            o = (acc[:, :HEAD] / acc[:, HEAD:]).astype(BF16)
            for g in range(GROUP):
                h = c * GROUP + g
                o_ref[:, h * HEAD : (h + 1) * HEAD] = o[g * ROWS : (g + 1) * ROWS]

    late = (s >= 8) & (r8 <= 2)

    @pl.when(jnp.logical_not(late))
    def _():
        take_two(V)
        finish_values()

    ar_b[0] = ar_finish(ar_a, stage_a)
    for c in stage_b:
        c.start()

    @pl.when(late)
    def _():
        take_two(V)

    ar_c[0] = ar_finish(ar_b, stage_b)
    for c in stage_c:
        c.start()

    @pl.when(late)
    def _():
        finish_values()

    head_max = ar_finish(ar_c, stage_c)
    clipped = CLIP / jnp.maximum(head_max, CLIP)
    spread = jnp.broadcast_to(clipped, (ROWS, ROWS))
    down = jnp.transpose(spread)
    group = lax.div(row, GROUP)
    big = jnp.full((ROWS, ROWS), jnp.inf, F32)
    per_query = jnp.min(jnp.where(group == lax.div(col, GROUP), down, big), axis=0, keepdims=True)
    per_key = jnp.min(
        jnp.where(group == jnp.minimum(col, KV_HEADS - 1), down, big), axis=0, keepdims=True
    )
    fac_ref[0:1, :] = clipped / jnp.sqrt(per_query)
    fac_ref[1:2, :] = jnp.sqrt(per_key)

    for copies in (stage_a, stage_b, stage_c):
        for c in copies:
            c.wait_send()
    for cond, make in flows.values():
        @pl.when(cond)
        def _():
            for i in (K, V):
                for h in range(CHUNKS):
                    make(i, h).wait_send()


def local(queries, keys, values, segments):
    width, kv_width = QUERY_HEADS * HEAD, KV_HEADS * HEAD
    hbm_spec = pl.BlockSpec(memory_space=pltpu.HBM)
    vmem_spec = pl.BlockSpec(memory_space=pltpu.VMEM)
    dma = pltpu.SemaphoreType.DMA
    attended, factors = pl.pallas_call(
        kernel,
        name="packed_attention",
        out_shape=(
            jax.ShapeDtypeStruct((ROWS, width), BF16),
            jax.ShapeDtypeStruct((2, ROWS), F32),
        ),
        in_specs=[hbm_spec, hbm_spec, hbm_spec, hbm_spec],
        out_specs=(vmem_spec, vmem_spec),
        scratch_shapes=[
            pltpu.VMEM((ROWS, width), BF16),
            pltpu.VMEM((4 * ROWS, kv_width), BF16),
            pltpu.VMEM((4 * ROWS, kv_width), BF16),
            pltpu.VMEM((2, ROWS, kv_width), BF16),
            pltpu.VMEM((4, ROWS, ROWS), F32),
            pltpu.VMEM((KV_HEADS, 4, GROUP * ROWS, ROWS), F32),
            pltpu.VMEM((KV_HEADS, GROUP * ROWS, ROWS), F32),
            pltpu.VMEM((KV_HEADS, GROUP * ROWS, 4 * ROWS), BF16),
            pltpu.VMEM(segments.shape, jnp.int32),
            pltpu.VMEM((ROWS, ROWS), F32),
            pltpu.VMEM((8, 1, ROWS), F32),
            pltpu.VMEM((8, 1, ROWS), F32),
            pltpu.VMEM((12, 1, ROWS), F32),
            dma((4,)),
            dma((6, 2, CHUNKS)),
            dma((4, 2, CHUNKS)),
            dma((8,)),
            dma((8,)),
            dma((8,)),
            dma((8,)),
            dma((12,)),
            dma((12,)),
        ],
        compiler_params=pltpu.CompilerParams(
            collective_id=0, has_side_effects=True, vmem_limit_bytes=48 * 1024 * 1024
        ),
    )(*(pltpu.with_memory_space_constraint(a, pltpu.HBM) for a in (queries[0], keys[0], values[0], segments)))
    return attended[None], factors[0, :QUERY_HEADS], factors[1, :KV_HEADS]


def solution(mesh):
    in_specs = (P("dp", "seq", None), P("dp", "seq", None), P("dp", "seq", None), P("dp", None))
    out_specs = (P("dp", "seq", None), P(), P())
    return jax.shard_map(local, mesh=mesh, in_specs=in_specs, out_specs=out_specs, check_vma=False)
```

```python
import functools
import math

import jax
import jax.numpy as jnp
from jax import lax
from jax.experimental import pallas as pl
from jax.experimental.pallas import tpu as pltpu
from jax.sharding import PartitionSpec as P

QUERY_HEADS = 48
KV_HEADS = 6
GROUP = QUERY_HEADS // KV_HEADS
HEAD = 128
ROWS = 128
CLIP = 6.0
NEG = -1e30
SCALE = HEAD**-0.5
CHUNKS = 4
CROWS = ROWS // CHUNKS
MESH = pl.DeviceIdType.MESH
BF16, F32 = jnp.bfloat16, jnp.float32

F1, F2, F34, F5, CROSS, RELAY = range(6)
R1, R2, R3, RB = range(4)


def kernel(
    q_hbm, k_hbm, v_hbm, seg_hbm, o_ref, hmax_ref,
    q_ref, kall, vall, relay, bias_ref, rm_ref, p_ref, seg_ref, hm_ref,
    ar_a, ar_b, ar_c,
    load_sem, send_sem, recv_sem, a_send, a_recv, b_send, b_recv, c_send, c_recv,
):
    dp, s = lax.axis_index("dp"), lax.axis_index("seq")
    core = lax.rem(s, 2)
    r8 = lax.rem(s, 8)
    zh = lax.div(s, 8)
    x = lax.div(r8, 2)
    y = lax.rem(dp, 8)
    zl = lax.div(dp, 8)
    z = zh * 4 + zl

    def dev_a(k):
        return (dp, zh * 8 + lax.rem(r8 + k, 8))

    def dev_b(k):
        return (zl * 8 + lax.rem(y + k, 8), s)

    def dev_c(k):
        zz = lax.rem(z + k, 12)
        return (lax.rem(zz, 4) * 8 + y, lax.div(zz, 4) * 8 + r8)

    load_seg = pltpu.make_async_copy(seg_hbm, seg_ref, load_sem.at[3])
    load_seg.start()
    barrier = pltpu.get_barrier_semaphore()
    for n, dev in ((8, dev_a), (8, dev_b), (12, dev_c)):
        for k in range(1, n):
            pl.semaphore_signal(barrier, inc=1, device_id=dev(k), device_id_type=MESH)

    @pl.when((x == 0) & (zh >= 1))
    def _():
        for back in (jnp.where(core == 0, 3, 2), 6):
            pl.semaphore_signal(barrier, inc=1, device_id=(dp, s - back), device_id_type=MESH)

    load_k = pltpu.make_async_copy(k_hbm, kall.at[pl.ds(3 * ROWS, ROWS)], load_sem.at[0])
    load_q = pltpu.make_async_copy(q_hbm, q_ref, load_sem.at[1])
    load_v = pltpu.make_async_copy(v_hbm, vall.at[pl.ds(3 * ROWS, ROWS)], load_sem.at[2])
    load_k.start()
    load_q.start()
    load_v.start()

    for d in (1, 2, 3):
        @pl.when(s < d)
        def _():
            zero = jnp.zeros((ROWS, KV_HEADS * HEAD), BF16)
            kall[pl.ds((3 - d) * ROWS, ROWS), :] = zero
            vall[pl.ds((3 - d) * ROWS, ROWS), :] = zero

    load_seg.wait()

    def seg_row(block):
        start = pl.multiple_of(jnp.maximum(block, 0) * ROWS, ROWS)
        return seg_ref[:, pl.ds(start, ROWS)].astype(F32)

    own = jnp.broadcast_to(seg_row(s), (ROWS, ROWS))
    query_doc = jnp.transpose(own)
    row = lax.broadcasted_iota(jnp.int32, (ROWS, ROWS), 0)
    col = lax.broadcasted_iota(jnp.int32, (ROWS, ROWS), 1)
    for t in range(4):
        key_doc = jnp.broadcast_to(seg_row(s - 3 + t), (ROWS, ROWS))
        gap = jnp.abs(key_doc - query_doc)
        if t == 3:
            gap = gap + jnp.maximum(col - row, 0).astype(F32)
        else:
            gap = gap + jnp.where(s - 3 + t < 0, 1.0, 0.0)
        bias_ref[t] = jnp.where(gap > 0.5, NEG, 0.0)
    hm_ref[...] = jnp.full((ROWS, ROWS), NEG, F32)

    def queries_of(c):
        base = c * (GROUP * HEAD)
        return jnp.concatenate(
            [
                q_ref[:, pl.ds(pl.multiple_of(base + g * HEAD, HEAD), HEAD)]
                for g in range(GROUP)
            ],
            axis=0,
        )

    def products(c, first, count):
        cols = pl.ds(pl.multiple_of(c * HEAD, HEAD), HEAD)
        kb = kall[pl.ds(first * ROWS, count * ROWS), cols]
        return lax.dot_general(
            queries_of(c), kb, (((1,), (1,)), ((), ())), preferred_element_type=F32
        )

    def s_blocks(first, count, last):
        def body(c, carry):
            lg = products(c, first, count)
            mx = None if first == 3 else rm_ref[c].reshape(GROUP, ROWS, ROWS)
            for n in range(count):
                t = first + n
                one = lg[:, n * ROWS : (n + 1) * ROWS].reshape(GROUP, ROWS, ROWS)
                one = one + bias_ref[t][None]
                mx = one if mx is None else jnp.maximum(mx, one)
            rm_ref[c] = mx.reshape(GROUP * ROWS, ROWS)
            if last:
                hm_ref[pl.ds(pl.multiple_of(c * GROUP, GROUP), GROUP), :] = jnp.max(mx, axis=1)
            return carry

        lax.fori_loop(0, KV_HEADS, body, 0)

    load_k.wait()
    load_q.wait()
    s_blocks(3, 1, False)
    load_v.wait()
    direct = (((core == 1) & (x >= 2)) | (x == 1)) & (zh <= 1)
    pl.semaphore_wait(barrier, 25 + jnp.where(direct, 1, 0))

    bufs = (kall, vall)

    def part(i, d, h):
        return bufs[i].at[pl.ds((3 - d) * ROWS + h * CROWS, CROWS)]

    def relay_part(i, h):
        return relay.at[i, pl.ds(h * CROWS, CROWS)]

    def copy(src, dst, kind, slot, i, h, target):
        return pltpu.make_async_remote_copy(
            src_ref=src,
            dst_ref=dst,
            send_sem=send_sem.at[kind, i, h],
            recv_sem=recv_sem.at[slot, i, h],
            device_id=(dp, target),
            device_id_type=MESH,
        )

    def await_part(slot, i, h):
        dst = relay_part(i, h) if slot == RB else part(i, slot + 1, h)
        copy(dst, dst, F1, slot, i, h, s).wait_recv()

    odd, even = core == 1, core == 0
    flows = {
        "f1": (even, lambda i, h: copy(part(i, 0, h), part(i, 1, h), F1, R1, i, h, s + 1)),
        "f2": (x <= 2, lambda i, h: copy(part(i, 0, h), part(i, 2, h), F2, R2, i, h, s + 2)),
        "f3": (even & (s >= 2), lambda i, h: copy(part(i, 2, h), part(i, 3, h), F34, R3, i, h, s + 1)),
        "f4": (odd & (s >= 2), lambda i, h: copy(part(i, 2, h), part(i, 1, h), F34, R1, i, h, s - 1)),
        "f5": (
            odd & (s >= 3) & (x <= 2),
            lambda i, h: copy(part(i, 2, h), part(i, 3, h), F5, R3, i, h, s + 1),
        ),
        "cross_7": (
            odd & (x == 3) & (zh <= 1),
            lambda i, h: copy(part(i, 0, h), part(i, 2, h), CROSS, R2, i, h, s + 2),
        ),
        "cross_5": (
            odd & (x == 2) & (zh <= 1),
            lambda i, h: copy(part(i, 0, h), part(i, 3, h), CROSS, R3, i, h, s + 3),
        ),
        "cross_6": (
            even & (x == 3) & (zh <= 1),
            lambda i, h: copy(part(i, 0, h), relay_part(i, h), CROSS, RB, i, h, s - 6),
        ),
        "side": (
            (x == 3) & (zh <= 1),
            lambda i, h: copy(part(i, 0, h), relay_part(i, h), CROSS, RB, i, h, s - 4),
        ),
        "relay_6": (
            even & (x == 0) & (zh <= 1),
            lambda i, h: copy(relay_part(i, h), part(i, 2, h), RELAY, R2, i, h, s + 8),
        ),
        "relay_1": (
            (x == 1) & (zh <= 1),
            lambda i, h: copy(relay_part(i, h), part(i, 2, h), RELAY, R2, i, h, s + 6),
        ),
    }
    every = tuple(range(CHUNKS))
    most, last = every[:-1], every[-1:]
    chunks_of = {"cross_7": most, "cross_6": most, "relay_6": most, "side": last, "relay_1": last}

    def start(name, i, h=None, also=None):
        cond, make = flows[name]
        if also is not None:
            cond = cond & also

        @pl.when(cond)
        def _():
            for j in chunks_of.get(name, every) if h is None else (h,):
                make(i, j).start()

    K, V = 0, 1

    def cross(i):
        start("side", i)
        start("cross_7", i)
        start("cross_5", i)
        start("cross_6", i)

    def take_relay(i):
        for name in ("relay_6", "relay_1"):
            cond, make = flows[name]
            for h in chunks_of[name]:
                @pl.when(cond)
                def _():
                    await_part(RB, i, h)
                    make(i, h).start()

    cross(K)
    start("f2", K)
    start("f1", K)
    start("f2", V, also=x == 0)
    start("f1", V, also=x == 0)
    take_relay(K)

    def take_two(i):
        for h in range(CHUNKS):
            @pl.when(s >= 2)
            def _():
                await_part(R2, i, h)
            start("f4", i, h)
            start("f3", i, h)
            start("f5", i, h)

    def take(slot, i):
        @pl.when(s >= slot + 1)
        def _():
            for h in range(CHUNKS):
                await_part(slot, i, h)

    take_two(K)
    start("f2", V, also=x > 0)
    start("f1", V, also=x > 0)
    take(R1, K)
    s_blocks(1, 2, False)
    take(R3, K)
    s_blocks(0, 1, True)
    cross(V)

    def ar_copies(buf, n, dev, sends, recvs):
        return [
            pltpu.make_async_remote_copy(
                src_ref=buf.at[0],
                dst_ref=buf.at[k],
                send_sem=sends.at[k],
                recv_sem=recvs.at[k],
                device_id=dev(k),
                device_id_type=MESH,
            )
            for k in range(1, n)
        ]

    def ar_finish(buf, copies):
        for c in copies:
            c.wait_recv()
        return jnp.max(buf[...], axis=0)

    stage_a = ar_copies(ar_a, 8, dev_a, a_send, a_recv)
    stage_b = ar_copies(ar_b, 8, dev_b, b_send, b_recv)
    stage_c = ar_copies(ar_c, 12, dev_c, c_send, c_recv)

    ar_a[0] = jnp.max(jnp.transpose(hm_ref[...]), axis=0, keepdims=True) * SCALE
    for c in stage_a:
        c.start()
    take_relay(V)

    def p_body(c, carry):
        m = jnp.max(rm_ref[c], axis=1, keepdims=True).reshape(GROUP, ROWS, 1)
        for first in (0, 2):
            lg = products(c, first, 2)
            for n in range(2):
                t = first + n
                one = lg[:, n * ROWS : (n + 1) * ROWS].reshape(GROUP, ROWS, ROWS)
                p = jnp.exp2(((one + bias_ref[t][None]) - m) * (SCALE * math.log2(math.e)))
                p_ref[c, :, t * ROWS : (t + 1) * ROWS] = p.astype(BF16).reshape(GROUP * ROWS, ROWS)
        return carry

    lax.fori_loop(0, KV_HEADS, p_body, 0)

    def finish_values():
        take(R1, V)
        take(R3, V)
        for c in range(KV_HEADS):
            vc = jnp.concatenate(
                [vall[:, c * HEAD : (c + 1) * HEAD], jnp.ones((4 * ROWS, HEAD), BF16)], axis=1
            )
            acc = jnp.dot(p_ref[c], vc, preferred_element_type=F32)
            o = (acc[:, :HEAD] / acc[:, HEAD:]).astype(BF16)
            for g in range(GROUP):
                h = c * GROUP + g
                o_ref[:, h * HEAD : (h + 1) * HEAD] = o[g * ROWS : (g + 1) * ROWS]

    late = (s >= 8) & (r8 <= 2)

    @pl.when(jnp.logical_not(late))
    def _():
        take_two(V)
        finish_values()

    ar_b[0] = ar_finish(ar_a, stage_a)
    for c in stage_b:
        c.start()

    @pl.when(late)
    def _():
        take_two(V)

    ar_c[0] = ar_finish(ar_b, stage_b)
    for c in stage_c:
        c.start()

    @pl.when(late)
    def _():
        finish_values()

    head_max = ar_finish(ar_c, stage_c)
    hmax_ref[...] = head_max

    for copies in (stage_a, stage_b, stage_c):
        for c in copies:
            c.wait_send()
    for name, (cond, make) in flows.items():
        @pl.when(cond)
        def _():
            for i in (K, V):
                for h in chunks_of.get(name, every):
                    make(i, h).wait_send()


def finish(o_ref, hmax_ref, out_hbm, query_ref, key_ref, sem):
    parts = 4
    copies = []
    for n in range(parts):
        rows = pl.ds(n * (ROWS // parts), ROWS // parts)
        copies.append(pltpu.make_async_copy(o_ref.at[rows], out_hbm.at[rows], sem.at[n]))
        copies[-1].start()
    clipped = CLIP / jnp.maximum(hmax_ref[...], CLIP)
    down = jnp.transpose(jnp.broadcast_to(clipped, (ROWS, ROWS)))
    group = lax.div(lax.broadcasted_iota(jnp.int32, (ROWS, ROWS), 0), GROUP)
    col = lax.broadcasted_iota(jnp.int32, (ROWS, ROWS), 1)
    big = jnp.full((ROWS, ROWS), jnp.inf, F32)
    per_query = jnp.min(jnp.where(group == lax.div(col, GROUP), down, big), axis=0, keepdims=True)
    per_key = jnp.min(
        jnp.where(group == jnp.minimum(col, KV_HEADS - 1), down, big), axis=0, keepdims=True
    )
    query_ref[...] = (clipped / jnp.sqrt(per_query))[:, :QUERY_HEADS]
    key_ref[...] = jnp.sqrt(per_key)[:, :KV_HEADS]
    for c in copies:
        c.wait()


def local(queries, keys, values, segments):
    width, kv_width = QUERY_HEADS * HEAD, KV_HEADS * HEAD
    hbm_spec = pl.BlockSpec(memory_space=pltpu.HBM)
    vmem_spec = pl.BlockSpec(memory_space=pltpu.VMEM)
    dma = pltpu.SemaphoreType.DMA
    mixed, head_max = pl.pallas_call(
        kernel,
        name="packed_attention",
        out_shape=(
            jax.ShapeDtypeStruct((ROWS, width), BF16),
            jax.ShapeDtypeStruct((1, ROWS), F32),
        ),
        in_specs=[hbm_spec, hbm_spec, hbm_spec, hbm_spec],
        out_specs=(vmem_spec, vmem_spec),
        scratch_shapes=[
            pltpu.VMEM((ROWS, width), BF16),
            pltpu.VMEM((4 * ROWS, kv_width), BF16),
            pltpu.VMEM((4 * ROWS, kv_width), BF16),
            pltpu.VMEM((2, ROWS, kv_width), BF16),
            pltpu.VMEM((4, ROWS, ROWS), F32),
            pltpu.VMEM((KV_HEADS, GROUP * ROWS, ROWS), F32),
            pltpu.VMEM((KV_HEADS, GROUP * ROWS, 4 * ROWS), BF16),
            pltpu.VMEM(segments.shape, jnp.int32),
            pltpu.VMEM((ROWS, ROWS), F32),
            pltpu.VMEM((8, 1, ROWS), F32),
            pltpu.VMEM((8, 1, ROWS), F32),
            pltpu.VMEM((12, 1, ROWS), F32),
            dma((4,)),
            dma((6, 2, CHUNKS)),
            dma((4, 2, CHUNKS)),
            dma((8,)),
            dma((8,)),
            dma((8,)),
            dma((8,)),
            dma((12,)),
            dma((12,)),
        ],
        compiler_params=pltpu.CompilerParams(
            collective_id=0, has_side_effects=True, vmem_limit_bytes=48 * 1024 * 1024
        ),
    )(*(pltpu.with_memory_space_constraint(a, pltpu.HBM) for a in (queries[0], keys[0], values[0], segments)))
    any_spec = pl.BlockSpec(memory_space=pl.ANY)
    attended, query_factor, key_head_factor = pl.pallas_call(
        finish,
        name="finish",
        out_shape=(
            jax.ShapeDtypeStruct((ROWS, width), BF16),
            jax.ShapeDtypeStruct((1, QUERY_HEADS), F32),
            jax.ShapeDtypeStruct((1, KV_HEADS), F32),
        ),
        in_specs=[any_spec, vmem_spec],
        out_specs=(any_spec, vmem_spec, vmem_spec),
        scratch_shapes=[dma((4,))],
        compiler_params=pltpu.CompilerParams(vmem_limit_bytes=8 * 1024 * 1024),
    )(mixed, head_max)
    return attended[None], query_factor[0], key_head_factor[0]


def solution(mesh):
    in_specs = (P("dp", "seq", None), P("dp", "seq", None), P("dp", "seq", None), P("dp", None))
    out_specs = (P("dp", "seq", None), P(), P())
    return jax.shard_map(local, mesh=mesh, in_specs=in_specs, out_specs=out_specs, check_vma=False)
```

```python
import functools
import math

import jax
import jax.numpy as jnp
from jax import lax
from jax.experimental import pallas as pl
from jax.experimental.pallas import tpu as pltpu
from jax.sharding import PartitionSpec as P

QUERY_HEADS = 48
KV_HEADS = 6
GROUP = QUERY_HEADS // KV_HEADS
HEAD = 128
ROWS = 128
CLIP = 6.0
NEG = -1e30
SCALE = HEAD**-0.5
CHUNKS = 4
CROWS = ROWS // CHUNKS
MESH = pl.DeviceIdType.MESH
BF16, F32 = jnp.bfloat16, jnp.float32

F1, F2, F34, F5, CROSS, RELAY = range(6)
R1, R2, R3, RB = range(4)


def kernel(
    q_hbm, k_hbm, v_hbm, seg_hbm, o_ref, hmax_ref,
    q_ref, kall, vall, relay, bias_ref, rm_ref, p_ref, seg_ref, hm_ref,
    ar_a, ar_b, ar_c,
    load_sem, send_sem, recv_sem, a_send, a_recv, b_send, b_recv, c_send, c_recv,
):
    dp, s = lax.axis_index("dp"), lax.axis_index("seq")
    core = lax.rem(s, 2)
    r8 = lax.rem(s, 8)
    zh = lax.div(s, 8)
    x = lax.div(r8, 2)
    y = lax.rem(dp, 8)
    zl = lax.div(dp, 8)
    z = zh * 4 + zl

    def dev_a(k):
        return (dp, zh * 8 + lax.rem(r8 + k, 8))

    def dev_b(k):
        return (zl * 8 + lax.rem(y + k, 8), s)

    def dev_c(k):
        zz = lax.rem(z + k, 12)
        return (lax.rem(zz, 4) * 8 + y, lax.div(zz, 4) * 8 + r8)

    load_seg = pltpu.make_async_copy(seg_hbm, seg_ref, load_sem.at[3])
    load_seg.start()
    barrier = pltpu.get_barrier_semaphore()
    for n, dev in ((8, dev_a), (8, dev_b), (12, dev_c)):
        for k in range(1, n):
            pl.semaphore_signal(barrier, inc=1, device_id=dev(k), device_id_type=MESH)

    @pl.when((x == 0) & (zh >= 1))
    def _():
        for back in (jnp.where(core == 0, 3, 2), 6):
            pl.semaphore_signal(barrier, inc=1, device_id=(dp, s - back), device_id_type=MESH)

    load_k = pltpu.make_async_copy(k_hbm, kall.at[pl.ds(3 * ROWS, ROWS)], load_sem.at[0])
    load_q = pltpu.make_async_copy(q_hbm, q_ref, load_sem.at[1])
    load_v = pltpu.make_async_copy(v_hbm, vall.at[pl.ds(3 * ROWS, ROWS)], load_sem.at[2])
    load_k.start()
    load_q.start()
    load_v.start()

    for d in (1, 2, 3):
        @pl.when(s < d)
        def _():
            zero = jnp.zeros((ROWS, KV_HEADS * HEAD), BF16)
            kall[pl.ds((3 - d) * ROWS, ROWS), :] = zero
            vall[pl.ds((3 - d) * ROWS, ROWS), :] = zero

    load_seg.wait()

    def seg_row(block):
        start = pl.multiple_of(jnp.maximum(block, 0) * ROWS, ROWS)
        return seg_ref[:, pl.ds(start, ROWS)].astype(F32)

    own = jnp.broadcast_to(seg_row(s), (ROWS, ROWS))
    query_doc = jnp.transpose(own)
    row = lax.broadcasted_iota(jnp.int32, (ROWS, ROWS), 0)
    col = lax.broadcasted_iota(jnp.int32, (ROWS, ROWS), 1)
    for t in range(4):
        key_doc = jnp.broadcast_to(seg_row(s - 3 + t), (ROWS, ROWS))
        gap = jnp.abs(key_doc - query_doc)
        if t == 3:
            gap = gap + jnp.maximum(col - row, 0).astype(F32)
        else:
            gap = gap + jnp.where(s - 3 + t < 0, 1.0, 0.0)
        bias_ref[t] = jnp.where(gap > 0.5, NEG, 0.0)
    hm_ref[...] = jnp.full((ROWS, ROWS), NEG, F32)

    def queries_of(c):
        base = c * (GROUP * HEAD)
        return jnp.concatenate(
            [
                q_ref[:, pl.ds(pl.multiple_of(base + g * HEAD, HEAD), HEAD)]
                for g in range(GROUP)
            ],
            axis=0,
        )

    def products(c, first, count):
        cols = pl.ds(pl.multiple_of(c * HEAD, HEAD), HEAD)
        kb = kall[pl.ds(first * ROWS, count * ROWS), cols]
        return lax.dot_general(
            queries_of(c), kb, (((1,), (1,)), ((), ())), preferred_element_type=F32
        )

    def s_blocks(first, count, last):
        def body(c, carry):
            lg = products(c, first, count)
            mx = None if first == 3 else rm_ref[c].reshape(GROUP, ROWS, ROWS)
            for n in range(count):
                t = first + n
                one = lg[:, n * ROWS : (n + 1) * ROWS].reshape(GROUP, ROWS, ROWS)
                one = one + bias_ref[t][None]
                mx = one if mx is None else jnp.maximum(mx, one)
            rm_ref[c] = mx.reshape(GROUP * ROWS, ROWS)
            if last:
                hm_ref[pl.ds(pl.multiple_of(c * GROUP, GROUP), GROUP), :] = jnp.max(mx, axis=1)
            return carry

        lax.fori_loop(0, KV_HEADS, body, 0)

    load_k.wait()
    load_q.wait()
    s_blocks(3, 1, False)
    load_v.wait()
    direct = (((core == 1) & (x >= 2)) | (x == 1)) & (zh <= 1)
    pl.semaphore_wait(barrier, 25 + jnp.where(direct, 1, 0))

    bufs = (kall, vall)

    def part(i, d, h):
        return bufs[i].at[pl.ds((3 - d) * ROWS + h * CROWS, CROWS)]

    def relay_part(i, h):
        return relay.at[i, pl.ds(h * CROWS, CROWS)]

    def copy(src, dst, kind, slot, i, h, target):
        return pltpu.make_async_remote_copy(
            src_ref=src,
            dst_ref=dst,
            send_sem=send_sem.at[kind, i, h],
            recv_sem=recv_sem.at[slot, i, h],
            device_id=(dp, target),
            device_id_type=MESH,
        )

    def await_part(slot, i, h):
        dst = relay_part(i, h) if slot == RB else part(i, slot + 1, h)
        copy(dst, dst, F1, slot, i, h, s).wait_recv()

    odd, even = core == 1, core == 0
    flows = {
        "f1": (even, lambda i, h: copy(part(i, 0, h), part(i, 1, h), F1, R1, i, h, s + 1)),
        "f2": (x <= 2, lambda i, h: copy(part(i, 0, h), part(i, 2, h), F2, R2, i, h, s + 2)),
        "f3": (even & (s >= 2), lambda i, h: copy(part(i, 2, h), part(i, 3, h), F34, R3, i, h, s + 1)),
        "f4": (odd & (s >= 2), lambda i, h: copy(part(i, 2, h), part(i, 1, h), F34, R1, i, h, s - 1)),
        "f5": (
            odd & (s >= 3) & (x <= 2),
            lambda i, h: copy(part(i, 2, h), part(i, 3, h), F5, R3, i, h, s + 1),
        ),
        "cross_7": (
            odd & (x == 3) & (zh <= 1),
            lambda i, h: copy(part(i, 0, h), part(i, 2, h), CROSS, R2, i, h, s + 2),
        ),
        "cross_5": (
            odd & (x == 2) & (zh <= 1),
            lambda i, h: copy(part(i, 0, h), part(i, 3, h), CROSS, R3, i, h, s + 3),
        ),
        "cross_6": (
            even & (x == 3) & (zh <= 1),
            lambda i, h: copy(part(i, 0, h), relay_part(i, h), CROSS, RB, i, h, s - 6),
        ),
        "side": (
            (x == 3) & (zh <= 1),
            lambda i, h: copy(part(i, 0, h), relay_part(i, h), CROSS, RB, i, h, s - 4),
        ),
        "relay_6": (
            even & (x == 0) & (zh <= 1),
            lambda i, h: copy(relay_part(i, h), part(i, 2, h), RELAY, R2, i, h, s + 8),
        ),
        "relay_1": (
            (x == 1) & (zh <= 1),
            lambda i, h: copy(relay_part(i, h), part(i, 2, h), RELAY, R2, i, h, s + 6),
        ),
    }
    every = tuple(range(CHUNKS))
    most, last = every[:-1], every[-1:]
    chunks_of = {"cross_7": most, "cross_6": most, "relay_6": most, "side": last, "relay_1": last}

    def start(name, i, h=None, also=None):
        cond, make = flows[name]
        if also is not None:
            cond = cond & also

        @pl.when(cond)
        def _():
            for j in chunks_of.get(name, every) if h is None else (h,):
                make(i, j).start()

    K, V = 0, 1

    def cross(i):
        start("side", i)
        start("cross_7", i)
        start("cross_5", i)
        start("cross_6", i)

    def take_relay(i, also):
        for name in ("relay_6", "relay_1"):
            cond, make = flows[name]
            for h in chunks_of[name]:
                @pl.when(cond & also)
                def _():
                    await_part(RB, i, h)
                    make(i, h).start()

    cross(K)
    start("f2", K)
    start("f1", K)
    start("f2", V, also=x == 0)
    start("f1", V, also=x == 0)
    take_relay(K, zh >= 0)

    def take_two(i):
        for h in range(CHUNKS):
            @pl.when(s >= 2)
            def _():
                await_part(R2, i, h)
            start("f4", i, h)
            start("f3", i, h)
            start("f5", i, h)

    def take(slot, i):
        @pl.when(s >= slot + 1)
        def _():
            for h in range(CHUNKS):
                await_part(slot, i, h)

    take_two(K)
    start("f2", V, also=x > 0)
    start("f1", V, also=x > 0)
    take(R1, K)
    s_blocks(1, 2, False)
    take(R3, K)
    s_blocks(0, 1, True)
    cross(V)

    def ar_copies(buf, n, dev, sends, recvs):
        return [
            pltpu.make_async_remote_copy(
                src_ref=buf.at[0],
                dst_ref=buf.at[k],
                send_sem=sends.at[k],
                recv_sem=recvs.at[k],
                device_id=dev(k),
                device_id_type=MESH,
            )
            for k in range(1, n)
        ]

    def ar_finish(buf, copies):
        for c in copies:
            c.wait_recv()
        return jnp.max(buf[...], axis=0)

    stage_a = ar_copies(ar_a, 8, dev_a, a_send, a_recv)
    stage_b = ar_copies(ar_b, 8, dev_b, b_send, b_recv)
    stage_c = ar_copies(ar_c, 12, dev_c, c_send, c_recv)

    ar_a[0] = jnp.max(jnp.transpose(hm_ref[...]), axis=0, keepdims=True) * SCALE
    for c in stage_a:
        c.start()

    def p_body(c, carry):
        m = jnp.max(rm_ref[c], axis=1, keepdims=True).reshape(GROUP, ROWS, 1)
        for first in (0, 2):
            lg = products(c, first, 2)
            for n in range(2):
                t = first + n
                one = lg[:, n * ROWS : (n + 1) * ROWS].reshape(GROUP, ROWS, ROWS)
                p = jnp.exp2(((one + bias_ref[t][None]) - m) * (SCALE * math.log2(math.e)))
                p_ref[c, :, t * ROWS : (t + 1) * ROWS] = p.astype(BF16).reshape(GROUP * ROWS, ROWS)
        return carry

    late = (s >= 8) & (r8 <= 2)
    half = KV_HEADS // 2
    take_relay(V, late)
    lax.fori_loop(0, half, p_body, 0)
    take_relay(V, jnp.logical_not(late))

    def finish_values():
        take(R1, V)
        take(R3, V)
        for c in range(KV_HEADS):
            vc = jnp.concatenate(
                [vall[:, c * HEAD : (c + 1) * HEAD], jnp.ones((4 * ROWS, HEAD), BF16)], axis=1
            )
            acc = jnp.dot(p_ref[c], vc, preferred_element_type=F32)
            o = (acc[:, :HEAD] / acc[:, HEAD:]).astype(BF16)
            for g in range(GROUP):
                h = c * GROUP + g
                o_ref[:, h * HEAD : (h + 1) * HEAD] = o[g * ROWS : (g + 1) * ROWS]

    @pl.when(jnp.logical_not(late))
    def _():
        lax.fori_loop(half, KV_HEADS, p_body, 0)
        take_two(V)

    @pl.when(x >= 2)
    def _():
        finish_values()

    ar_b[0] = ar_finish(ar_a, stage_a)
    for c in stage_b:
        c.start()

    @pl.when(late)
    def _():
        lax.fori_loop(half, KV_HEADS, p_body, 0)
        take_two(V)

    ar_c[0] = ar_finish(ar_b, stage_b)
    for c in stage_c:
        c.start()

    @pl.when(x <= 1)
    def _():
        finish_values()

    head_max = ar_finish(ar_c, stage_c)
    hmax_ref[...] = head_max

    for copies in (stage_a, stage_b, stage_c):
        for c in copies:
            c.wait_send()
    for name, (cond, make) in flows.items():
        @pl.when(cond)
        def _():
            for i in (K, V):
                for h in chunks_of.get(name, every):
                    make(i, h).wait_send()


def finish(o_ref, hmax_ref, out_hbm, query_ref, key_ref, sem):
    parts = 4
    copies = []
    for n in range(parts):
        rows = pl.ds(n * (ROWS // parts), ROWS // parts)
        copies.append(pltpu.make_async_copy(o_ref.at[rows], out_hbm.at[rows], sem.at[n]))
        copies[-1].start()
    clipped = CLIP / jnp.maximum(hmax_ref[...], CLIP)
    down = jnp.transpose(jnp.broadcast_to(clipped, (ROWS, ROWS)))
    group = lax.div(lax.broadcasted_iota(jnp.int32, (ROWS, ROWS), 0), GROUP)
    col = lax.broadcasted_iota(jnp.int32, (ROWS, ROWS), 1)
    big = jnp.full((ROWS, ROWS), jnp.inf, F32)
    per_query = jnp.min(jnp.where(group == lax.div(col, GROUP), down, big), axis=0, keepdims=True)
    per_key = jnp.min(
        jnp.where(group == jnp.minimum(col, KV_HEADS - 1), down, big), axis=0, keepdims=True
    )
    query_ref[...] = (clipped / jnp.sqrt(per_query))[:, :QUERY_HEADS]
    key_ref[...] = jnp.sqrt(per_key)[:, :KV_HEADS]
    for c in copies:
        c.wait()


def local(queries, keys, values, segments):
    width, kv_width = QUERY_HEADS * HEAD, KV_HEADS * HEAD
    hbm_spec = pl.BlockSpec(memory_space=pltpu.HBM)
    vmem_spec = pl.BlockSpec(memory_space=pltpu.VMEM)
    dma = pltpu.SemaphoreType.DMA
    mixed, head_max = pl.pallas_call(
        kernel,
        name="packed_attention",
        out_shape=(
            jax.ShapeDtypeStruct((ROWS, width), BF16),
            jax.ShapeDtypeStruct((1, ROWS), F32),
        ),
        in_specs=[hbm_spec, hbm_spec, hbm_spec, hbm_spec],
        out_specs=(vmem_spec, vmem_spec),
        scratch_shapes=[
            pltpu.VMEM((ROWS, width), BF16),
            pltpu.VMEM((4 * ROWS, kv_width), BF16),
            pltpu.VMEM((4 * ROWS, kv_width), BF16),
            pltpu.VMEM((2, ROWS, kv_width), BF16),
            pltpu.VMEM((4, ROWS, ROWS), F32),
            pltpu.VMEM((KV_HEADS, GROUP * ROWS, ROWS), F32),
            pltpu.VMEM((KV_HEADS, GROUP * ROWS, 4 * ROWS), BF16),
            pltpu.VMEM(segments.shape, jnp.int32),
            pltpu.VMEM((ROWS, ROWS), F32),
            pltpu.VMEM((8, 1, ROWS), F32),
            pltpu.VMEM((8, 1, ROWS), F32),
            pltpu.VMEM((12, 1, ROWS), F32),
            dma((4,)),
            dma((6, 2, CHUNKS)),
            dma((4, 2, CHUNKS)),
            dma((8,)),
            dma((8,)),
            dma((8,)),
            dma((8,)),
            dma((12,)),
            dma((12,)),
        ],
        compiler_params=pltpu.CompilerParams(
            collective_id=0, has_side_effects=True, vmem_limit_bytes=48 * 1024 * 1024
        ),
    )(*(pltpu.with_memory_space_constraint(a, pltpu.HBM) for a in (queries[0], keys[0], values[0], segments)))
    any_spec = pl.BlockSpec(memory_space=pl.ANY)
    attended, query_factor, key_head_factor = pl.pallas_call(
        finish,
        name="finish",
        out_shape=(
            jax.ShapeDtypeStruct((ROWS, width), BF16),
            jax.ShapeDtypeStruct((1, QUERY_HEADS), F32),
            jax.ShapeDtypeStruct((1, KV_HEADS), F32),
        ),
        in_specs=[any_spec, vmem_spec],
        out_specs=(any_spec, vmem_spec, vmem_spec),
        scratch_shapes=[dma((4,))],
        compiler_params=pltpu.CompilerParams(vmem_limit_bytes=8 * 1024 * 1024),
    )(mixed, head_max)
    return attended[None], query_factor[0], key_head_factor[0]


def solution(mesh):
    in_specs = (P("dp", "seq", None), P("dp", "seq", None), P("dp", "seq", None), P("dp", None))
    out_specs = (P("dp", "seq", None), P(), P())
    return jax.shard_map(local, mesh=mesh, in_specs=in_specs, out_specs=out_specs, check_vma=False)
```

```python
import functools
import math

import jax
import jax.numpy as jnp
from jax import lax
from jax.experimental import pallas as pl
from jax.experimental.pallas import tpu as pltpu
from jax.sharding import PartitionSpec as P

QUERY_HEADS = 48
KV_HEADS = 6
GROUP = QUERY_HEADS // KV_HEADS
HEAD = 128
ROWS = 128
CLIP = 6.0
NEG = -1e30
SCALE = HEAD**-0.5
CHUNKS = 4
CROWS = ROWS // CHUNKS
MESH = pl.DeviceIdType.MESH
BF16, F32 = jnp.bfloat16, jnp.float32

F1, F2, F34, F5, CROSS, RELAY = range(6)
R1, R2, R3, RB = range(4)


def far_first(n):
    return sorted(range(1, n), key=lambda k: abs(2 * k - n))


def kernel(
    q_hbm, k_hbm, v_hbm, seg_hbm, o_ref, hmax_ref,
    q_ref, kall, vall, relay, bias_ref, rm_ref, p_ref, seg_ref, hm_ref,
    ar_a, ar_b, ar_c,
    load_sem, send_sem, recv_sem, a_send, a_recv, b_send, b_recv, c_send, c_recv,
):
    dp, s = lax.axis_index("dp"), lax.axis_index("seq")
    core = lax.rem(s, 2)
    r8 = lax.rem(s, 8)
    zh = lax.div(s, 8)
    x = lax.div(r8, 2)
    y = lax.rem(dp, 8)
    zl = lax.div(dp, 8)
    z = zh * 4 + zl

    def dev_a(k):
        return (dp, zh * 8 + lax.rem(r8 + k, 8))

    def dev_b(k):
        return (zl * 8 + lax.rem(y + k, 8), s)

    def dev_c(k):
        zz = lax.rem(z + k, 12)
        return (lax.rem(zz, 4) * 8 + y, lax.div(zz, 4) * 8 + r8)

    load_seg = pltpu.make_async_copy(seg_hbm, seg_ref, load_sem.at[3])
    load_seg.start()
    barrier = pltpu.get_barrier_semaphore()
    @pl.when((x == 0) & (zh >= 1))
    def _():
        for back in (jnp.where(core == 0, 3, 2), 6):
            pl.semaphore_signal(barrier, inc=1, device_id=(dp, s - back), device_id_type=MESH)

    for n, dev in ((12, dev_c), (8, dev_b), (8, dev_a)):
        for k in far_first(n):
            pl.semaphore_signal(barrier, inc=1, device_id=dev(k), device_id_type=MESH)

    load_k = pltpu.make_async_copy(k_hbm, kall.at[pl.ds(3 * ROWS, ROWS)], load_sem.at[0])
    load_q = pltpu.make_async_copy(q_hbm, q_ref, load_sem.at[1])
    load_v = pltpu.make_async_copy(v_hbm, vall.at[pl.ds(3 * ROWS, ROWS)], load_sem.at[2])
    load_k.start()
    load_q.start()
    load_v.start()

    for d in (1, 2, 3):
        @pl.when(s < d)
        def _():
            zero = jnp.zeros((ROWS, KV_HEADS * HEAD), BF16)
            kall[pl.ds((3 - d) * ROWS, ROWS), :] = zero
            vall[pl.ds((3 - d) * ROWS, ROWS), :] = zero

    load_seg.wait()

    def seg_row(block):
        start = pl.multiple_of(jnp.maximum(block, 0) * ROWS, ROWS)
        return seg_ref[:, pl.ds(start, ROWS)].astype(F32)

    own = jnp.broadcast_to(seg_row(s), (ROWS, ROWS))
    query_doc = jnp.transpose(own)
    row = lax.broadcasted_iota(jnp.int32, (ROWS, ROWS), 0)
    col = lax.broadcasted_iota(jnp.int32, (ROWS, ROWS), 1)
    for t in range(4):
        key_doc = jnp.broadcast_to(seg_row(s - 3 + t), (ROWS, ROWS))
        gap = jnp.abs(key_doc - query_doc)
        if t == 3:
            gap = gap + jnp.maximum(col - row, 0).astype(F32)
        else:
            gap = gap + jnp.where(s - 3 + t < 0, 1.0, 0.0)
        bias_ref[t] = jnp.where(gap > 0.5, NEG, 0.0)
    hm_ref[...] = jnp.full((ROWS, ROWS), NEG, F32)

    def queries_of(c):
        base = c * (GROUP * HEAD)
        return jnp.concatenate(
            [
                q_ref[:, pl.ds(pl.multiple_of(base + g * HEAD, HEAD), HEAD)]
                for g in range(GROUP)
            ],
            axis=0,
        )

    def products(c, first, count):
        cols = pl.ds(pl.multiple_of(c * HEAD, HEAD), HEAD)
        kb = kall[pl.ds(first * ROWS, count * ROWS), cols]
        return lax.dot_general(
            queries_of(c), kb, (((1,), (1,)), ((), ())), preferred_element_type=F32
        )

    def s_blocks(first, count, last):
        def body(c, carry):
            lg = products(c, first, count)
            mx = None if first == 3 else rm_ref[c].reshape(GROUP, ROWS, ROWS)
            for n in range(count):
                t = first + n
                one = lg[:, n * ROWS : (n + 1) * ROWS].reshape(GROUP, ROWS, ROWS)
                one = one + bias_ref[t][None]
                mx = one if mx is None else jnp.maximum(mx, one)
            rm_ref[c] = mx.reshape(GROUP * ROWS, ROWS)
            if last:
                hm_ref[pl.ds(pl.multiple_of(c * GROUP, GROUP), GROUP), :] = jnp.max(mx, axis=1)
            return carry

        lax.fori_loop(0, KV_HEADS, body, 0)

    load_k.wait()
    load_q.wait()
    s_blocks(3, 1, False)
    load_v.wait()
    direct = (((core == 1) & (x >= 2)) | (x == 1)) & (zh <= 1)
    pl.semaphore_wait(barrier, 25 + jnp.where(direct, 1, 0))

    bufs = (kall, vall)

    def part(i, d, h):
        return bufs[i].at[pl.ds((3 - d) * ROWS + h * CROWS, CROWS)]

    def relay_part(i, h):
        return relay.at[i, pl.ds(h * CROWS, CROWS)]

    def copy(src, dst, kind, slot, i, h, target):
        return pltpu.make_async_remote_copy(
            src_ref=src,
            dst_ref=dst,
            send_sem=send_sem.at[kind, i, h],
            recv_sem=recv_sem.at[slot, i, h],
            device_id=(dp, target),
            device_id_type=MESH,
        )

    def await_part(slot, i, h):
        dst = relay_part(i, h) if slot == RB else part(i, slot + 1, h)
        copy(dst, dst, F1, slot, i, h, s).wait_recv()

    odd, even = core == 1, core == 0
    flows = {
        "f1": (even, lambda i, h: copy(part(i, 0, h), part(i, 1, h), F1, R1, i, h, s + 1)),
        "f2": (x <= 2, lambda i, h: copy(part(i, 0, h), part(i, 2, h), F2, R2, i, h, s + 2)),
        "f3": (even & (s >= 2), lambda i, h: copy(part(i, 2, h), part(i, 3, h), F34, R3, i, h, s + 1)),
        "f4": (odd & (s >= 2), lambda i, h: copy(part(i, 2, h), part(i, 1, h), F34, R1, i, h, s - 1)),
        "f5": (
            odd & (s >= 3) & (x <= 2),
            lambda i, h: copy(part(i, 2, h), part(i, 3, h), F5, R3, i, h, s + 1),
        ),
        "cross_7": (
            odd & (x == 3) & (zh <= 1),
            lambda i, h: copy(part(i, 0, h), part(i, 2, h), CROSS, R2, i, h, s + 2),
        ),
        "cross_5": (
            odd & (x == 2) & (zh <= 1),
            lambda i, h: copy(part(i, 0, h), part(i, 3, h), CROSS, R3, i, h, s + 3),
        ),
        "cross_6": (
            even & (x == 3) & (zh <= 1),
            lambda i, h: copy(part(i, 0, h), relay_part(i, h), CROSS, RB, i, h, s - 6),
        ),
        "side": (
            (x == 3) & (zh <= 1),
            lambda i, h: copy(part(i, 0, h), relay_part(i, h), CROSS, RB, i, h, s - 4),
        ),
        "relay_6": (
            even & (x == 0) & (zh <= 1),
            lambda i, h: copy(relay_part(i, h), part(i, 2, h), RELAY, R2, i, h, s + 8),
        ),
        "relay_1": (
            (x == 1) & (zh <= 1),
            lambda i, h: copy(relay_part(i, h), part(i, 2, h), RELAY, R2, i, h, s + 6),
        ),
    }
    every = tuple(range(CHUNKS))
    most, last = every[:-1], every[-1:]
    chunks_of = {"cross_7": most, "cross_6": most, "relay_6": most, "side": last, "relay_1": last}

    def start(name, i, h=None, also=None):
        cond, make = flows[name]
        if also is not None:
            cond = cond & also

        @pl.when(cond)
        def _():
            for j in chunks_of.get(name, every) if h is None else (h,):
                make(i, j).start()

    K, V = 0, 1

    def cross(i):
        start("side", i)
        start("cross_7", i)
        start("cross_5", i)
        start("cross_6", i)

    def take_relay(i, also):
        for name in ("relay_6", "relay_1"):
            cond, make = flows[name]
            for h in chunks_of[name]:
                @pl.when(cond & also)
                def _():
                    await_part(RB, i, h)
                    make(i, h).start()

    cross(K)
    start("f2", K)
    start("f1", K)
    start("f2", V, also=x == 0)
    start("f1", V, also=x == 0)
    take_relay(K, zh >= 0)

    def take_two(i):
        for h in range(CHUNKS):
            @pl.when(s >= 2)
            def _():
                await_part(R2, i, h)
            start("f4", i, h)
            start("f3", i, h)
            start("f5", i, h)

    def take(slot, i):
        @pl.when(s >= slot + 1)
        def _():
            for h in range(CHUNKS):
                await_part(slot, i, h)

    take_two(K)
    start("f2", V, also=x > 0)
    start("f1", V, also=x > 0)
    take(R1, K)
    s_blocks(1, 2, False)
    take(R3, K)
    s_blocks(0, 1, True)
    cross(V)

    def ar_copies(buf, n, dev, sends, recvs):
        return [
            pltpu.make_async_remote_copy(
                src_ref=buf.at[0],
                dst_ref=buf.at[k],
                send_sem=sends.at[k],
                recv_sem=recvs.at[k],
                device_id=dev(k),
                device_id_type=MESH,
            )
            for k in far_first(n)
        ]

    def ar_finish(buf, copies):
        for c in copies:
            c.wait_recv()
        return jnp.max(buf[...], axis=0)

    stage_a = ar_copies(ar_a, 8, dev_a, a_send, a_recv)
    stage_b = ar_copies(ar_b, 8, dev_b, b_send, b_recv)
    stage_c = ar_copies(ar_c, 12, dev_c, c_send, c_recv)

    ar_a[0] = jnp.max(jnp.transpose(hm_ref[...]), axis=0, keepdims=True) * SCALE
    for c in stage_a:
        c.start()

    def p_body(c, carry):
        m = jnp.max(rm_ref[c], axis=1, keepdims=True).reshape(GROUP, ROWS, 1)
        for first in (0, 2):
            lg = products(c, first, 2)
            for n in range(2):
                t = first + n
                one = lg[:, n * ROWS : (n + 1) * ROWS].reshape(GROUP, ROWS, ROWS)
                p = jnp.exp2(((one + bias_ref[t][None]) - m) * (SCALE * math.log2(math.e)))
                p_ref[c, :, t * ROWS : (t + 1) * ROWS] = p.astype(BF16).reshape(GROUP * ROWS, ROWS)
        return carry

    late = (s >= 8) & (r8 <= 2)
    half = KV_HEADS // 2
    take_relay(V, late)
    lax.fori_loop(0, half, p_body, 0)
    take_relay(V, jnp.logical_not(late))

    def finish_values():
        take(R1, V)
        take(R3, V)
        for c in range(KV_HEADS):
            vc = jnp.concatenate(
                [vall[:, c * HEAD : (c + 1) * HEAD], jnp.ones((4 * ROWS, HEAD), BF16)], axis=1
            )
            acc = jnp.dot(p_ref[c], vc, preferred_element_type=F32)
            o = (acc[:, :HEAD] / acc[:, HEAD:]).astype(BF16)
            for g in range(GROUP):
                h = c * GROUP + g
                o_ref[:, h * HEAD : (h + 1) * HEAD] = o[g * ROWS : (g + 1) * ROWS]

    @pl.when(jnp.logical_not(late))
    def _():
        lax.fori_loop(half, KV_HEADS, p_body, 0)
        take_two(V)

    @pl.when(x >= 2)
    def _():
        finish_values()

    ar_b[0] = ar_finish(ar_a, stage_a)
    for c in stage_b:
        c.start()

    @pl.when(late)
    def _():
        lax.fori_loop(half, KV_HEADS, p_body, 0)
        take_two(V)

    ar_c[0] = ar_finish(ar_b, stage_b)
    for c in stage_c:
        c.start()

    @pl.when(x <= 1)
    def _():
        finish_values()

    head_max = ar_finish(ar_c, stage_c)
    hmax_ref[...] = head_max

    for copies in (stage_a, stage_b, stage_c):
        for c in copies:
            c.wait_send()
    for name, (cond, make) in flows.items():
        @pl.when(cond)
        def _():
            for i in (K, V):
                for h in chunks_of.get(name, every):
                    make(i, h).wait_send()


def finish(o_ref, hmax_ref, out_hbm, query_ref, key_ref, sem):
    parts = 4
    copies = []
    for n in range(parts):
        rows = pl.ds(n * (ROWS // parts), ROWS // parts)
        copies.append(pltpu.make_async_copy(o_ref.at[rows], out_hbm.at[rows], sem.at[n]))
        copies[-1].start()
    clipped = CLIP / jnp.maximum(hmax_ref[...], CLIP)
    down = jnp.transpose(jnp.broadcast_to(clipped, (ROWS, ROWS)))
    group = lax.div(lax.broadcasted_iota(jnp.int32, (ROWS, ROWS), 0), GROUP)
    col = lax.broadcasted_iota(jnp.int32, (ROWS, ROWS), 1)
    big = jnp.full((ROWS, ROWS), jnp.inf, F32)
    per_query = jnp.min(jnp.where(group == lax.div(col, GROUP), down, big), axis=0, keepdims=True)
    per_key = jnp.min(
        jnp.where(group == jnp.minimum(col, KV_HEADS - 1), down, big), axis=0, keepdims=True
    )
    query_ref[...] = (clipped / jnp.sqrt(per_query))[:, :QUERY_HEADS]
    key_ref[...] = jnp.sqrt(per_key)[:, :KV_HEADS]
    for c in copies:
        c.wait()


def local(queries, keys, values, segments):
    width, kv_width = QUERY_HEADS * HEAD, KV_HEADS * HEAD
    hbm_spec = pl.BlockSpec(memory_space=pltpu.HBM)
    vmem_spec = pl.BlockSpec(memory_space=pltpu.VMEM)
    dma = pltpu.SemaphoreType.DMA
    mixed, head_max = pl.pallas_call(
        kernel,
        name="packed_attention",
        out_shape=(
            jax.ShapeDtypeStruct((ROWS, width), BF16),
            jax.ShapeDtypeStruct((1, ROWS), F32),
        ),
        in_specs=[hbm_spec, hbm_spec, hbm_spec, hbm_spec],
        out_specs=(vmem_spec, vmem_spec),
        scratch_shapes=[
            pltpu.VMEM((ROWS, width), BF16),
            pltpu.VMEM((4 * ROWS, kv_width), BF16),
            pltpu.VMEM((4 * ROWS, kv_width), BF16),
            pltpu.VMEM((2, ROWS, kv_width), BF16),
            pltpu.VMEM((4, ROWS, ROWS), F32),
            pltpu.VMEM((KV_HEADS, GROUP * ROWS, ROWS), F32),
            pltpu.VMEM((KV_HEADS, GROUP * ROWS, 4 * ROWS), BF16),
            pltpu.VMEM(segments.shape, jnp.int32),
            pltpu.VMEM((ROWS, ROWS), F32),
            pltpu.VMEM((8, 1, ROWS), F32),
            pltpu.VMEM((8, 1, ROWS), F32),
            pltpu.VMEM((12, 1, ROWS), F32),
            dma((4,)),
            dma((6, 2, CHUNKS)),
            dma((4, 2, CHUNKS)),
            dma((8,)),
            dma((8,)),
            dma((8,)),
            dma((8,)),
            dma((12,)),
            dma((12,)),
        ],
        compiler_params=pltpu.CompilerParams(
            collective_id=0, has_side_effects=True, vmem_limit_bytes=48 * 1024 * 1024
        ),
    )(*(pltpu.with_memory_space_constraint(a, pltpu.HBM) for a in (queries[0], keys[0], values[0], segments)))
    any_spec = pl.BlockSpec(memory_space=pl.ANY)
    attended, query_factor, key_head_factor = pl.pallas_call(
        finish,
        name="finish",
        out_shape=(
            jax.ShapeDtypeStruct((ROWS, width), BF16),
            jax.ShapeDtypeStruct((1, QUERY_HEADS), F32),
            jax.ShapeDtypeStruct((1, KV_HEADS), F32),
        ),
        in_specs=[any_spec, vmem_spec],
        out_specs=(any_spec, vmem_spec, vmem_spec),
        scratch_shapes=[dma((4,))],
        compiler_params=pltpu.CompilerParams(vmem_limit_bytes=8 * 1024 * 1024),
    )(mixed, head_max)
    return attended[None], query_factor[0], key_head_factor[0]


def solution(mesh):
    in_specs = (P("dp", "seq", None), P("dp", "seq", None), P("dp", "seq", None), P("dp", None))
    out_specs = (P("dp", "seq", None), P(), P())
    return jax.shard_map(local, mesh=mesh, in_specs=in_specs, out_specs=out_specs, check_vma=False)
```
